1024 devices in a mesh: pipe: 64 (over z, x_hi, core), dp: 16 (over x_lo, y).
Axes of the slice: x: 8 (x_hi: 4, x_lo: 2; x = x_hi * 2 + x_lo), y: 8, z: 8, core: 2. Of those that a mesh axis runs over, the one named last changes fastest.
Arguments:
- saved: bfloat16 [64, 4096, 1024], P('pipe', 'dp'), may hold values from -6 to 6
- passed: bfloat16 [64, 4096, 1024], P('pipe', 'dp'), may hold values from -6 to 6
- weight: bfloat16 [64, 1024, 1024], P('pipe'), may hold values from -0.1875 to 0.1875
- master: float32 [64, 1024, 1024], P('pipe', 'dp'), may hold values from -0.1875 to 0.1875
- moment_one: float32 [64, 1024, 1024], P('pipe', 'dp'), may hold values from -6 to 6
- moment_two: float32 [64, 1024, 1024], P('pipe', 'dp'), may hold values from 0.5 to 4
- counts: int32 [32], P('dp'), may hold values from 1 to 128, 3072 in all
Outputs:
- input_grad: bfloat16 [64, 4096, 1024], P('pipe', 'dp')
- master_new: float32 [64, 1024, 1024], P('pipe', 'dp')
- moment_one_new: float32 [64, 1024, 1024], P('pipe', 'dp')
- moment_two_new: float32 [64, 1024, 1024], P('pipe', 'dp')
The draws below stay inside these ranges and needn't reach their ends.
Inputs may be any that keep to these rules, and one draw needn't show every extreme that they name: `counts`: each count is at most 128, and some micro-batch has all 128 slots live.
All inputs are finite; a program needn't handle non-finite values. No bound on the sum of `counts` on one device may be relied on, other than what follows from the above.
Results may differ from the reference program's by a relative error of at most 0.0049.
Values may be sent and summed in bfloat16 or wider, within the bound.
No kernel may reach another device: no remote copies, remote signals or barrier semaphores. Data moves between devices by JAX's collectives and lax.ppermute only.
A program may use at most 32 MiB of HBM per device.

```python
import math
import jax
import jax.numpy as jnp
import numpy as np
from jax import lax

D = 1024
MB = 2
ROWS = 128
SECTIONS = 64
SLOTS = 4096
N_DP = 16


def levels(key, shape, split, least, top_value):
    loudness, own = 1.0, jax.random.fold_in(key, 6)
    for axis_at, blocks in split:
        steps = jnp.exp(jax.random.uniform(jax.random.fold_in(own, axis_at), (blocks,), jnp.float32, least / len(split), top_value / len(split)))
        loudness = loudness * jnp.repeat(steps, shape[axis_at] // blocks).reshape([-1 if axis == axis_at else 1 for axis in range(len(shape))])
    return loudness


def split_up(count, total, limit, lean):
    weights = [(1 << 20) // math.isqrt(grade ** lean) + 1 for grade in range(2, count + 1)]
    spare, given = total - limit - (count - 1), [1] * (count - 1)
    while spare > 0:
        movable = [i for i in range(count - 1) if given[i] < limit]
        pool, remaining = sum([weights[i] for i in movable]), spare
        for i in movable:
            more = min(limit - given[i], max(1, remaining * weights[i] // pool), spare)
            given[i] = given[i] + more
            spare = spare - more
    return np.array([limit] + given)


def uneven(key, number_of, total, limit, skew):
    if number_of == 2:
        one = jax.random.randint(key, (), max(1, total - limit), min(limit, total - 1) + 1)
        return jnp.stack([one, total - one])
    lengths = jnp.asarray(split_up(number_of, total, limit, skew), jnp.int32)
    pairs = (number_of - 1) // 2
    source_of, receiver = lengths[1:1 + 2 * pairs:2], lengths[2:2 + 2 * pairs:2]
    room = jnp.minimum(source_of - 1, limit - receiver)
    shifted = jax.random.randint(jax.random.fold_in(key, 1), (pairs,), 0, 1 << 20) % (room + 1)
    lengths = lengths.at[1:1 + 2 * pairs:2].set(source_of - shifted).at[2:2 + 2 * pairs:2].set(receiver + shifted)
    return lengths[jax.random.permutation(jax.random.fold_in(key, 2), number_of)]


def noise(own_key, extent, width, reach, pieces=(), held_as=jnp.bfloat16):
    entries = jax.random.normal(own_key, extent, jnp.float32) * width
    if len(pieces) > 0:
        entries = levels(own_key, extent, pieces, -0.22, 0.18) * entries
    return jnp.clip(entries, min=-reach, max=reach).astype(held_as)


def setup_inputs(seed: int = 0) -> dict:
    key_list = jax.random.split(jax.random.key(seed), 8)
    saved = noise(key_list[0], (SECTIONS, SLOTS, D), 1.0, 6.0, ((0, 64), (1, 16)))
    passed = noise(key_list[1], (SECTIONS, SLOTS, D), 1.0, 6.0, ((0, 64), (1, 16)))
    weight = noise(key_list[2], (SECTIONS, D, D), D ** -0.5, 0.1875, ((0, 64),))
    master = noise(key_list[3], (SECTIONS, D, D), D ** -0.5, 0.1875, ((0, 64), (1, 16)), jnp.float32)
    moment_one = noise(key_list[4], (SECTIONS, D, D), 1.0, 6.0, ((0, 64), (1, 16)), jnp.float32)
    moment_two = jnp.clip(jnp.exp(math.log(4.0) - 2.0794415 * jax.random.uniform(key_list[5], (SECTIONS, D, D), jnp.float32) ** levels(key_list[5], (SECTIONS, D, D), ((0, 64), (1, 16)), -0.2, 0.2)), 0.5, 4.0)
    counts = uneven(key_list[6], N_DP * MB, N_DP * MB * ROWS * 3 // 4, ROWS, 2).astype(jnp.int32)
    return {"saved": saved, "passed": passed, "weight": weight, "master": master, "moment_one": moment_one, "moment_two": moment_two, "counts": counts}


corr_first = 0.9999734386011124
corr_second = 0.09520785288696

def reference(saved, passed, weight, master, moment_one, moment_two, counts):
    slots = saved.shape[1]
    live = jnp.arange(slots) % ROWS < jnp.repeat(counts, ROWS)
    upstream = jnp.roll(passed, -1, axis=0)
    scale = 1.0 / math.sqrt(slots)

    def section(items):
        acts, cot, w_section, master_section, first, second = items
        pre = jnp.dot(acts, w_section, preferred_element_type=jnp.float32)
        _, back = jax.vjp(jax.nn.gelu, pre)
        local_grad = back(cot.astype(jnp.float32))[0]
        local_grad = jnp.where(live[:, None], local_grad, jnp.float32(0.0)).astype(jnp.bfloat16)
        in_grad = lax.dot_general(local_grad, w_section, (((1,), (1,)), ((), ())), preferred_element_type=jnp.float32).astype(jnp.bfloat16)
        grad = lax.dot_general(acts, local_grad, (((0,), (0,)), ((), ())), preferred_element_type=jnp.float32) * scale
        first_new = 0.9 * first + 0.1 * grad
        second_new = 0.999 * second + 0.001 * grad * grad
        direction = first_new / corr_first / (jnp.sqrt(second_new / corr_second) + 1e-08)
        master_out = master_section - 0.01 * (direction + 0.1 * master_section)
        return (in_grad, master_out, first_new, second_new)
    return lax.map(section, (saved, upstream, weight, master, moment_one, moment_two))
```

```python
import math

import jax
import jax.numpy as jnp
from jax import lax
from jax.experimental import pallas as pl
from jax.experimental.pallas import tpu as pltpu
from jax.sharding import Mesh
from jax.sharding import PartitionSpec as P

corr_first = 0.9999734386011124
corr_second = 0.09520785288696
X_LO = 2
PAD = 7


def passed_along(x, axis, by):
    size = lax.axis_size(axis)
    return lax.ppermute(x, axis, [(i, (i + by) % size) for i in range(size)])


def weight_term(up_ref, slope_ref, acts_t_ref, lg_ref, total_ref):
    lg = (up_ref[...].astype(jnp.float32) * slope_ref[...]).astype(jnp.bfloat16)
    lg_ref[...] = lg
    total_ref[...] = jnp.dot(acts_t_ref[...], lg, preferred_element_type=jnp.float32).astype(jnp.bfloat16)


def local(saved, passed, weight, master, moment_one, moment_two, counts):
    acts = saved[0]
    w_section = weight[0]
    rows, width = acts.shape
    columns = lax.axis_size("y")
    owned = width // (X_LO * columns)
    upstream = passed_along(passed, "pipe", -1)[0]

    block = rows // counts.shape[0]
    live = jnp.arange(rows) % block < jnp.repeat(counts, block)
    pre = jnp.dot(acts, w_section, preferred_element_type=jnp.float32)
    _, back = jax.vjp(jax.nn.gelu, pre)
    slope = jnp.where(live[:, None], back(jnp.ones_like(pre))[0], jnp.float32(0.0))
    acts_t = acts.T.reshape(X_LO, columns, owned, rows).transpose(1, 0, 2, 3).reshape(columns, X_LO * owned, rows)
    acts_t = jnp.pad(acts_t, ((0, 0), (0, PAD), (0, 0))).reshape(-1, rows)

    vmem = pl.BlockSpec(memory_space=pltpu.VMEM)
    local_grad, total = pl.pallas_call(
        weight_term,
        out_shape=(
            jax.ShapeDtypeStruct((rows, width), jnp.bfloat16),
            jax.ShapeDtypeStruct((acts_t.shape[0], width), jnp.bfloat16),
        ),
        in_specs=[vmem] * 3,
        out_specs=(vmem, vmem),
        compiler_params=pltpu.CompilerParams(vmem_limit_bytes=24 * 1024 * 1024),
        name="weight_term",
    )(upstream, slope, acts_t)

    along_y = lax.optimization_barrier(lax.psum_scatter(total, "y", scatter_dimension=0, tiled=True))
    x_lo = lax.axis_index("x_lo")
    mine = lax.dynamic_slice_in_dim(along_y, x_lo * owned, owned, 0)
    other = lax.dynamic_slice_in_dim(along_y, (1 - x_lo) * owned, owned, 0)
    summed = mine.astype(jnp.float32) + passed_along(other, "x_lo", 1).astype(jnp.float32)

    in_grad = lax.dot_general(
        local_grad, w_section, (((1,), (1,)), ((), ())), preferred_element_type=jnp.float32
    ).astype(jnp.bfloat16)

    grad = summed * (1.0 / math.sqrt(X_LO * columns * rows))
    master_section = master[0]
    first_new = 0.9 * moment_one[0] + 0.1 * grad
    second_new = 0.999 * moment_two[0] + 0.001 * grad * grad
    direction = first_new / corr_first / (jnp.sqrt(second_new / corr_second) + 1e-08)
    master_out = master_section - 0.01 * (direction + 0.1 * master_section)
    return (in_grad[None], master_out[None], first_new[None], second_new[None])


def solution(mesh):
    pipe, dp = mesh.devices.shape
    split = Mesh(mesh.devices.reshape(pipe, X_LO, dp // X_LO), ("pipe", "x_lo", "y"))
    rows = ("x_lo", "y")
    in_specs = (
        P("pipe", rows, None),
        P("pipe", rows, None),
        P("pipe", None, None),
        P("pipe", rows, None),
        P("pipe", rows, None),
        P("pipe", rows, None),
        P(rows),
    )
    out_specs = (
        P("pipe", rows, None),
        P("pipe", rows, None),
        P("pipe", rows, None),
        P("pipe", rows, None),
    )
    return jax.shard_map(local, mesh=split, in_specs=in_specs, out_specs=out_specs, check_vma=False)
```

```python
import math

import jax
import jax.numpy as jnp
from jax import lax
from jax.experimental import pallas as pl
from jax.experimental.pallas import tpu as pltpu
from jax.sharding import Mesh
from jax.sharding import PartitionSpec as P


corr_first = 0.9999734386011124
corr_second = 0.09520785288696
X_LO = 2
PAD = 7
VMEM = pl.BlockSpec(memory_space=pltpu.VMEM)


def weight_term(up_ref, slope_ref, acts_t_ref, lg_ref, total_ref):
    lg = (up_ref[...].astype(jnp.float32) * slope_ref[...]).astype(jnp.bfloat16)
    lg_ref[...] = lg
    total_ref[...] = jnp.dot(acts_t_ref[...], lg, preferred_element_type=jnp.float32).astype(jnp.bfloat16)


def input_term(lg_ref, w_ref, in_grad_ref):
    in_grad_ref[...] = lax.dot_general(
        lg_ref[...], w_ref[...], (((1,), (1,)), ((), ())), preferred_element_type=jnp.float32
    ).astype(jnp.bfloat16)


def gradients(upstream, slope, acts_t, w_section):
    rows, width = upstream.shape
    owned = width // (X_LO * lax.axis_size("y"))
    local_grad, total = pl.pallas_call(
        weight_term,
        out_shape=(
            jax.ShapeDtypeStruct((rows, width), jnp.bfloat16),
            jax.ShapeDtypeStruct((acts_t.shape[0], width), jnp.bfloat16),
        ),
        in_specs=[VMEM] * 3,
        out_specs=(VMEM, VMEM),
        compiler_params=pltpu.CompilerParams(vmem_limit_bytes=24 * 1024 * 1024),
        name="weight_term",
    )(upstream, slope, acts_t)
    along_y = lax.optimization_barrier(lax.psum_scatter(total, "y", scatter_dimension=0, tiled=True))
    x_lo = lax.axis_index("x_lo")
    mine = lax.dynamic_slice_in_dim(along_y, x_lo * owned, owned, 0)
    other = lax.dynamic_slice_in_dim(along_y, (1 - x_lo) * owned, owned, 0)
    swapped = lax.ppermute(other, "x_lo", [(0, 1), (1, 0)])
    in_grad = pl.pallas_call(
        input_term,
        out_shape=jax.ShapeDtypeStruct((rows, width), jnp.bfloat16),
        in_specs=[VMEM] * 2,
        out_specs=VMEM,
        cost_estimate=pl.CostEstimate(flops=2 * rows * width * width, bytes_accessed=3 << 20, transcendentals=0),
        compiler_params=pltpu.CompilerParams(vmem_limit_bytes=24 * 1024 * 1024),
        name="input_term",
    )(local_grad, w_section)
    return in_grad, mine.astype(jnp.float32) + swapped.astype(jnp.float32)


def local(saved, passed, weight, master, moment_one, moment_two, counts):
    acts = saved[0]
    w_section = weight[0]
    rows, width = acts.shape
    sections, columns = lax.axis_size("pipe"), lax.axis_size("y")
    owned = width // (X_LO * columns)
    near = lax.ppermute(passed[0], "pipe", [(s, s - 1) for s in range(1, sections, 2)])
    far = lax.ppermute(passed[0], "pipe", [(s, (s - 1) % sections) for s in range(0, sections, 2)])

    block = rows // counts.shape[0]
    live = jnp.arange(rows) % block < jnp.repeat(counts, block)
    pre = jnp.dot(acts, w_section, preferred_element_type=jnp.float32)
    _, back = jax.vjp(jax.nn.gelu, pre)
    slope = jnp.where(live[:, None], back(jnp.ones_like(pre))[0], jnp.float32(0.0))
    acts_t = acts.T.reshape(X_LO, columns, owned, rows).transpose(1, 0, 2, 3).reshape(columns, X_LO * owned, rows)
    acts_t = jnp.pad(acts_t, ((0, 0), (0, PAD), (0, 0))).reshape(-1, rows)

    even = lax.axis_index("pipe") % 2 == 0
    done = lax.cond(
        even,
        lambda: gradients(near, slope, acts_t, w_section),
        lambda: (jnp.zeros((rows, width), jnp.bfloat16), jnp.zeros((owned, width), jnp.float32)),
    )
    in_grad, summed = lax.cond(even, lambda: done, lambda: gradients(far, slope, acts_t, w_section))

    grad = summed * (1.0 / math.sqrt(X_LO * columns * rows))
    master_section = master[0]
    first_new = 0.9 * moment_one[0] + 0.1 * grad
    second_new = 0.999 * moment_two[0] + 0.001 * grad * grad
    direction = first_new / corr_first / (jnp.sqrt(second_new / corr_second) + 1e-08)
    master_out = master_section - 0.01 * (direction + 0.1 * master_section)
    return (in_grad[None], master_out[None], first_new[None], second_new[None])


def solution(mesh):
    pipe, dp = mesh.devices.shape
    split = Mesh(mesh.devices.reshape(pipe, X_LO, dp // X_LO), ("pipe", "x_lo", "y"))
    rows = ("x_lo", "y")
    in_specs = (
        P("pipe", rows, None),
        P("pipe", rows, None),
        P("pipe", None, None),
        P("pipe", rows, None),
        P("pipe", rows, None),
        P("pipe", rows, None),
        P(rows),
    )
    out_specs = (
        P("pipe", rows, None),
        P("pipe", rows, None),
        P("pipe", rows, None),
        P("pipe", rows, None),
    )
    return jax.shard_map(local, mesh=split, in_specs=in_specs, out_specs=out_specs, check_vma=False)
```

```python
import math

import jax
import jax.numpy as jnp
from jax import lax
from jax.experimental import pallas as pl
from jax.experimental.pallas import tpu as pltpu
from jax.sharding import Mesh
from jax.sharding import PartitionSpec as P


corr_first = 0.9999734386011124
corr_second = 0.09520785288696
X_LO = 2
COLUMNS = 8
SPACER = 8
VMEM = pl.BlockSpec(memory_space=pltpu.VMEM)


def prepare(counts_ref, acts_ref, w_ref, slope_ref, acts_t_ref):
    rows, width = acts_ref.shape
    batches = counts_ref.shape[0]
    block = rows // batches
    owned, stride = width // (X_LO * COLUMNS), width // COLUMNS + SPACER
    acts = acts_ref[...]
    acts_t = acts.T
    for y in range(COLUMNS):
        for x_lo in range(X_LO):
            to, at = y * stride + x_lo * owned, x_lo * (width // X_LO) + y * owned
            acts_t_ref[to : to + owned, :] = acts_t[at : at + owned, :]
        if y < COLUMNS - 1:
            acts_t_ref[y * stride + X_LO * owned : (y + 1) * stride, :] = jnp.zeros((SPACER, rows), acts.dtype)
    for b in range(batches):
        at = slice(b * block, (b + 1) * block)
        pre = jnp.dot(acts[at, :], w_ref[...], preferred_element_type=jnp.float32)
        _, back = jax.vjp(jax.nn.gelu, pre)
        live = lax.broadcasted_iota(jnp.int32, pre.shape, 0) < counts_ref[b]
        slope_ref[at, :] = jnp.where(live, back(jnp.ones_like(pre))[0], jnp.float32(0.0))


def weight_term(up_ref, slope_ref, acts_t_ref, lg_ref, total_ref):
    lg = (up_ref[...].astype(jnp.float32) * slope_ref[...]).astype(jnp.bfloat16)
    lg_ref[...] = lg
    total_ref[...] = jnp.dot(acts_t_ref[...], lg, preferred_element_type=jnp.float32).astype(jnp.bfloat16)


def input_term(lg_ref, w_ref, in_grad_ref):
    in_grad_ref[...] = lax.dot_general(
        lg_ref[...], w_ref[...], (((1,), (1,)), ((), ())), preferred_element_type=jnp.float32
    ).astype(jnp.bfloat16)


def gradients(upstream, slope, acts_t, w_section):
    rows, width = upstream.shape
    owned = width // (X_LO * COLUMNS)
    local_grad, total = pl.pallas_call(
        weight_term,
        out_shape=(
            jax.ShapeDtypeStruct((rows, width), jnp.bfloat16),
            jax.ShapeDtypeStruct((acts_t.shape[0], width), jnp.bfloat16),
        ),
        in_specs=[VMEM] * 3,
        out_specs=(VMEM, VMEM),
        compiler_params=pltpu.CompilerParams(vmem_limit_bytes=24 * 1024 * 1024),
        name="weight_term",
    )(upstream, slope, acts_t)
    along_y = lax.optimization_barrier(lax.psum_scatter(total, "y", scatter_dimension=0, tiled=True))
    x_lo, y = lax.axis_index("x_lo"), lax.axis_index("y")
    mine = lax.dynamic_slice_in_dim(along_y, y + x_lo * owned, owned, 0)
    other = lax.dynamic_slice_in_dim(along_y, y + (1 - x_lo) * owned, owned, 0)
    swapped = lax.dynamic_index_in_dim(lax.all_gather(other, "x_lo"), 1 - x_lo, 0, keepdims=False)
    in_grad = pl.pallas_call(
        input_term,
        out_shape=jax.ShapeDtypeStruct((rows, width), jnp.bfloat16),
        in_specs=[VMEM] * 2,
        out_specs=VMEM,
        cost_estimate=pl.CostEstimate(flops=2 * rows * width * width, bytes_accessed=3 << 20, transcendentals=0),
        compiler_params=pltpu.CompilerParams(vmem_limit_bytes=24 * 1024 * 1024),
        name="input_term",
    )(local_grad, w_section)
    return in_grad, mine.astype(jnp.float32) + swapped.astype(jnp.float32)


def local(saved, passed, weight, master, moment_one, moment_two, counts):
    acts = saved[0]
    w_section = weight[0]
    rows, width = acts.shape
    sections = lax.axis_size("pipe")
    owned = width // (X_LO * COLUMNS)
    near = lax.ppermute(passed[0], "pipe", [(s, s - 1) for s in range(1, sections, 2)])
    far = lax.ppermute(passed[0], "pipe", [(s, (s - 1) % sections) for s in range(0, sections, 2)])

    slope, acts_t = pl.pallas_call(
        prepare,
        out_shape=(
            jax.ShapeDtypeStruct((rows, width), jnp.float32),
            jax.ShapeDtypeStruct((width + (COLUMNS - 1) * SPACER, rows), jnp.bfloat16),
        ),
        in_specs=[pl.BlockSpec(memory_space=pltpu.SMEM), VMEM, VMEM],
        out_specs=(VMEM, VMEM),
        compiler_params=pltpu.CompilerParams(vmem_limit_bytes=24 * 1024 * 1024),
        name="prepare",
    )(counts, acts, w_section)

    even = lax.axis_index("pipe") % 2 == 0
    done = lax.cond(
        even,
        lambda: gradients(near, slope, acts_t, w_section),
        lambda: (jnp.zeros((rows, width), jnp.bfloat16), jnp.zeros((owned, width), jnp.float32)),
    )
    in_grad, summed = lax.cond(even, lambda: done, lambda: gradients(far, slope, acts_t, w_section))

    grad = summed * (1.0 / math.sqrt(X_LO * COLUMNS * rows))
    master_section = master[0]
    first_new = 0.9 * moment_one[0] + 0.1 * grad
    second_new = 0.999 * moment_two[0] + 0.001 * grad * grad
    direction = first_new / corr_first / (jnp.sqrt(second_new / corr_second) + 1e-08)
    master_out = master_section - 0.01 * (direction + 0.1 * master_section)
    return (in_grad[None], master_out[None], first_new[None], second_new[None])


def solution(mesh):
    pipe = mesh.devices.shape[0]
    split = Mesh(mesh.devices.reshape(pipe, X_LO, COLUMNS), ("pipe", "x_lo", "y"))
    rows = ("x_lo", "y")
    in_specs = (
        P("pipe", rows, None),
        P("pipe", rows, None),
        P("pipe", None, None),
        P("pipe", rows, None),
        P("pipe", rows, None),
        P("pipe", rows, None),
        P(rows),
    )
    out_specs = (
        P("pipe", rows, None),
        P("pipe", rows, None),
        P("pipe", rows, None),
        P("pipe", rows, None),
    )
    return jax.shard_map(local, mesh=split, in_specs=in_specs, out_specs=out_specs, check_vma=False)
```

```python
import math

import jax
import jax.numpy as jnp
from jax import lax
from jax.experimental import pallas as pl
from jax.experimental.pallas import tpu as pltpu
from jax.sharding import Mesh
from jax.sharding import PartitionSpec as P


corr_first = 0.9999734386011124
corr_second = 0.09520785288696
X_LO = 2
COLUMNS = 8
SPACER = 8
VMEM = pl.BlockSpec(memory_space=pltpu.VMEM)


def prepare(counts_ref, acts_ref, w_ref, slope_ref, acts_t_ref):
    rows, width = acts_ref.shape
    batches = counts_ref.shape[0]
    block = rows // batches
    owned, stride = width // (X_LO * COLUMNS), width // COLUMNS + SPACER
    acts = acts_ref[...]
    acts_t = acts.T
    for y in range(COLUMNS):
        for x_lo in range(X_LO):
            to, at = y * stride + x_lo * owned, x_lo * (width // X_LO) + y * owned
            acts_t_ref[to : to + owned, :] = acts_t[at : at + owned, :]
        if y < COLUMNS - 1:
            acts_t_ref[y * stride + X_LO * owned : (y + 1) * stride, :] = jnp.zeros((SPACER, rows), acts.dtype)
    for b in range(batches):
        at = slice(b * block, (b + 1) * block)
        pre = jnp.dot(acts[at, :], w_ref[...], preferred_element_type=jnp.float32)
        _, back = jax.vjp(jax.nn.gelu, pre)
        live = lax.broadcasted_iota(jnp.int32, pre.shape, 0) < counts_ref[b]
        slope_ref[at, :] = jnp.where(live, back(jnp.ones_like(pre))[0], jnp.float32(0.0))


def weight_term(up_ref, slope_ref, acts_t_ref, lg_ref, total_ref):
    lg = (up_ref[...].astype(jnp.float32) * slope_ref[...]).astype(jnp.bfloat16)
    lg_ref[...] = lg
    total_ref[...] = jnp.dot(acts_t_ref[...], lg, preferred_element_type=jnp.float32).astype(jnp.bfloat16)


def input_term(lg_ref, w_ref, in_grad_ref):
    in_grad_ref[...] = lax.dot_general(
        lg_ref[...], w_ref[...], (((1,), (1,)), ((), ())), preferred_element_type=jnp.float32
    ).astype(jnp.bfloat16)


def unwritten(ref):
    del ref


def blank(shape, dtype):
    return pl.pallas_call(
        unwritten, out_shape=jax.ShapeDtypeStruct(shape, dtype), out_specs=pl.BlockSpec(memory_space=pl.ANY), name="blank"
    )()


def prepared(counts, acts, w_section):
    rows, width = acts.shape
    return pl.pallas_call(
        prepare,
        out_shape=(
            jax.ShapeDtypeStruct((rows, width), jnp.float32),
            jax.ShapeDtypeStruct((width + (COLUMNS - 1) * SPACER, rows), jnp.bfloat16),
        ),
        in_specs=[pl.BlockSpec(memory_space=pltpu.SMEM), VMEM, VMEM],
        out_specs=(VMEM, VMEM),
        compiler_params=pltpu.CompilerParams(vmem_limit_bytes=24 * 1024 * 1024),
        name="prepare",
    )(counts, acts, w_section)


def weight_gradient(upstream, slope, acts_t):
    rows, width = upstream.shape
    return pl.pallas_call(
        weight_term,
        out_shape=(
            jax.ShapeDtypeStruct((rows, width), jnp.bfloat16),
            jax.ShapeDtypeStruct((acts_t.shape[0], width), jnp.bfloat16),
        ),
        in_specs=[VMEM] * 3,
        out_specs=(VMEM, VMEM),
        compiler_params=pltpu.CompilerParams(vmem_limit_bytes=24 * 1024 * 1024),
        name="weight_term",
    )(upstream, slope, acts_t)


def input_gradient(local_grad, w_section):
    rows, width = local_grad.shape
    return pl.pallas_call(
        input_term,
        out_shape=jax.ShapeDtypeStruct((rows, width), jnp.bfloat16),
        in_specs=[VMEM] * 2,
        out_specs=VMEM,
        cost_estimate=pl.CostEstimate(flops=2 * rows * width * width, bytes_accessed=3 << 20, transcendentals=0),
        compiler_params=pltpu.CompilerParams(vmem_limit_bytes=24 * 1024 * 1024),
        name="input_term",
    )(local_grad, w_section)


def updated(total, master_section, first, second, slots):
    owned = total.shape[1] // (X_LO * COLUMNS)
    along_y = lax.optimization_barrier(lax.psum_scatter(total, "y", scatter_dimension=0, tiled=True))
    x_lo, y = lax.axis_index("x_lo"), lax.axis_index("y")
    mine = lax.dynamic_slice_in_dim(along_y, y + x_lo * owned, owned, 0)
    other = lax.dynamic_slice_in_dim(along_y, y + (1 - x_lo) * owned, owned, 0)
    swapped = lax.dynamic_index_in_dim(lax.all_gather(other, "x_lo"), 1 - x_lo, 0, keepdims=False)
    summed = mine.astype(jnp.float32) + swapped.astype(jnp.float32)
    grad = summed * (1.0 / math.sqrt(slots))
    first_new = 0.9 * first + 0.1 * grad
    second_new = 0.999 * second + 0.001 * grad * grad
    direction = first_new / corr_first / (jnp.sqrt(second_new / corr_second) + 1e-08)
    master_out = master_section - 0.01 * (direction + 0.1 * master_section)
    return master_out, first_new, second_new


def local(saved, passed, weight, master, moment_one, moment_two, counts):
    acts, w_section, block = saved[0], weight[0], passed[0]
    rows, width = acts.shape
    sections = lax.axis_size("pipe")
    section = lax.axis_index("pipe")
    slots = X_LO * COLUMNS * rows
    parts = (master[0], moment_one[0], moment_two[0])
    padded = width + (COLUMNS - 1) * SPACER

    def chain(upstream, slope, acts_t):
        local_grad, total = weight_gradient(upstream, slope, acts_t)
        new = updated(total, *parts, slots)
        return (input_gradient(local_grad, w_section), *new)

    def first_front(upstream):
        local_grad, total = weight_gradient(upstream, *prepared(counts, acts, w_section))
        return input_gradient(local_grad, w_section), total

    def nothing():
        return (blank((rows, width), jnp.bfloat16), *(blank(p.shape, p.dtype) for p in parts))

    own = lax.ppermute(block, "pipe", [(1, 0)])
    front = lax.cond(
        section == 0,
        first_front,
        lambda _: (blank((rows, width), jnp.bfloat16), blank((padded, width), jnp.bfloat16)),
        own,
    )
    far = lax.ppermute(block, "pipe", [(s, (s - 1) % sections) for s in range(0, sections, 2)])
    near = lax.ppermute(block, "pipe", [(s, s - 1) for s in range(3, sections, 2)])
    slope, acts_t = lax.cond(
        section == 0,
        lambda *_: (blank((rows, width), jnp.float32), blank((padded, rows), jnp.bfloat16)),
        prepared,
        counts,
        acts,
        w_section,
    )
    kind = jnp.where(section == 0, 0, 1 + section % 2)
    even = lax.switch(
        kind,
        (
            lambda: (front[0], *updated(front[1], *parts, slots)),
            lambda: chain(near, slope, acts_t),
            nothing,
        ),
    )
    out = lax.cond(section % 2 == 0, lambda: even, lambda: chain(far, slope, acts_t))
    return tuple(x[None] for x in out)


def solution(mesh):
    pipe = mesh.devices.shape[0]
    split = Mesh(mesh.devices.reshape(pipe, X_LO, COLUMNS), ("pipe", "x_lo", "y"))
    rows = ("x_lo", "y")
    in_specs = (
        P("pipe", rows, None),
        P("pipe", rows, None),
        P("pipe", None, None),
        P("pipe", rows, None),
        P("pipe", rows, None),
        P("pipe", rows, None),
        P(rows),
    )
    out_specs = (
        P("pipe", rows, None),
        P("pipe", rows, None),
        P("pipe", rows, None),
        P("pipe", rows, None),
    )
    return jax.shard_map(local, mesh=split, in_specs=in_specs, out_specs=out_specs, check_vma=False)
```

```python
import math

import jax
import jax.numpy as jnp
from jax import lax
from jax.experimental import pallas as pl
from jax.experimental.pallas import tpu as pltpu
from jax.sharding import Mesh
from jax.sharding import PartitionSpec as P


corr_first = 0.9999734386011124
corr_second = 0.09520785288696
X_LO = 2
COLUMNS = 8
SPACER = 8
VMEM = pl.BlockSpec(memory_space=pltpu.VMEM)


def prepare(counts_ref, acts_ref, w_ref, slope_ref, acts_t_ref):
    rows, width = acts_ref.shape
    batches = counts_ref.shape[0]
    block = rows // batches
    owned, stride = width // (X_LO * COLUMNS), width // COLUMNS + SPACER
    acts = acts_ref[...]
    acts_t = acts.T
    for y in range(COLUMNS):
        for x_lo in range(X_LO):
            to, at = y * stride + x_lo * owned, x_lo * (width // X_LO) + y * owned
            acts_t_ref[to : to + owned, :] = acts_t[at : at + owned, :]
        if y < COLUMNS - 1:
            acts_t_ref[y * stride + X_LO * owned : (y + 1) * stride, :] = jnp.zeros((SPACER, rows), acts.dtype)
    for b in range(batches):
        at = slice(b * block, (b + 1) * block)
        pre = jnp.dot(acts[at, :], w_ref[...], preferred_element_type=jnp.float32)
        _, back = jax.vjp(jax.nn.gelu, pre)
        live = lax.broadcasted_iota(jnp.int32, pre.shape, 0) < counts_ref[b]
        slope_ref[at, :] = jnp.where(live, back(jnp.ones_like(pre))[0], jnp.float32(0.0))


def weight_term(up_ref, slope_ref, acts_t_ref, lg_ref, total_ref):
    lg = (up_ref[...].astype(jnp.float32) * slope_ref[...]).astype(jnp.bfloat16)
    lg_ref[...] = lg
    total_ref[...] = jnp.dot(acts_t_ref[...], lg, preferred_element_type=jnp.float32).astype(jnp.bfloat16)


def input_term(lg_ref, w_ref, in_grad_ref):
    in_grad_ref[...] = lax.dot_general(
        lg_ref[...], w_ref[...], (((1,), (1,)), ((), ())), preferred_element_type=jnp.float32
    ).astype(jnp.bfloat16)


def unwritten(ref):
    del ref


def blank(shape, dtype):
    return pl.pallas_call(
        unwritten, out_shape=jax.ShapeDtypeStruct(shape, dtype), out_specs=pl.BlockSpec(memory_space=pl.ANY), name="blank"
    )()


def prepared(counts, acts, w_section):
    rows, width = acts.shape
    return pl.pallas_call(
        prepare,
        out_shape=(
            jax.ShapeDtypeStruct((rows, width), jnp.float32),
            jax.ShapeDtypeStruct((width + (COLUMNS - 1) * SPACER, rows), jnp.bfloat16),
        ),
        in_specs=[pl.BlockSpec(memory_space=pltpu.SMEM), VMEM, VMEM],
        out_specs=(VMEM, VMEM),
        compiler_params=pltpu.CompilerParams(vmem_limit_bytes=24 * 1024 * 1024),
        name="prepare",
    )(counts, acts, w_section)


def weight_gradient(upstream, slope, acts_t):
    rows, width = upstream.shape
    return pl.pallas_call(
        weight_term,
        out_shape=(
            jax.ShapeDtypeStruct((rows, width), jnp.bfloat16),
            jax.ShapeDtypeStruct((acts_t.shape[0], width), jnp.bfloat16),
        ),
        in_specs=[VMEM] * 3,
        out_specs=(VMEM, VMEM),
        compiler_params=pltpu.CompilerParams(vmem_limit_bytes=24 * 1024 * 1024),
        name="weight_term",
    )(upstream, slope, acts_t)


def input_gradient(local_grad, w_section):
    rows, width = local_grad.shape
    return pl.pallas_call(
        input_term,
        out_shape=jax.ShapeDtypeStruct((rows, width), jnp.bfloat16),
        in_specs=[VMEM] * 2,
        out_specs=VMEM,
        cost_estimate=pl.CostEstimate(flops=2 * rows * width * width, bytes_accessed=3 << 20, transcendentals=0),
        compiler_params=pltpu.CompilerParams(vmem_limit_bytes=24 * 1024 * 1024),
        name="input_term",
    )(local_grad, w_section)


def updated(total, master_section, first, second, slots):
    owned = total.shape[1] // (X_LO * COLUMNS)
    along_y = lax.optimization_barrier(lax.psum_scatter(total, "y", scatter_dimension=0, tiled=True))
    x_lo, y = lax.axis_index("x_lo"), lax.axis_index("y")
    mine = lax.dynamic_slice_in_dim(along_y, y + x_lo * owned, owned, 0)
    other = lax.dynamic_slice_in_dim(along_y, y + (1 - x_lo) * owned, owned, 0)
    swapped = lax.dynamic_index_in_dim(lax.all_gather(other, "x_lo"), 1 - x_lo, 0, keepdims=False)
    summed = mine.astype(jnp.float32) + swapped.astype(jnp.float32)
    grad = summed * (1.0 / math.sqrt(slots))
    first_new = 0.9 * first + 0.1 * grad
    second_new = 0.999 * second + 0.001 * grad * grad
    direction = first_new / corr_first / (jnp.sqrt(second_new / corr_second) + 1e-08)
    master_out = master_section - 0.01 * (direction + 0.1 * master_section)
    return master_out, first_new, second_new


def local(saved, passed, weight, master, moment_one, moment_two, counts):
    acts, w_section, block = saved[0], weight[0], passed[0]
    rows, width = acts.shape
    sections = lax.axis_size("pipe")
    section = lax.axis_index("pipe")
    slots = X_LO * COLUMNS * rows
    parts = (master[0], moment_one[0], moment_two[0])
    padded = width + (COLUMNS - 1) * SPACER

    def chain(upstream, slope, acts_t):
        local_grad, total = weight_gradient(upstream, slope, acts_t)
        new = updated(total, *parts, slots)
        return (input_gradient(local_grad, w_section), *new)

    def first_front(upstream):
        local_grad, total = weight_gradient(upstream, *prepared(counts, acts, w_section))
        return input_gradient(local_grad, w_section), total

    def nothing():
        return (blank((rows, width), jnp.bfloat16), *(blank(p.shape, p.dtype) for p in parts))

    far = lax.ppermute(block, "pipe", [(s, s - 1) for s in range(2, sections, 2)])
    own = lax.ppermute(block, "pipe", [(1, 0)])
    front = lax.cond(
        section == 0,
        first_front,
        lambda _: (blank((rows, width), jnp.bfloat16), blank((padded, width), jnp.bfloat16)),
        own,
    )
    around = lax.ppermute(block, "pipe", [(0, sections - 1)])
    near = lax.ppermute(block, "pipe", [(s, s - 1) for s in range(3, sections, 2)])
    slope, acts_t = lax.cond(
        section == 0,
        lambda *_: (blank((rows, width), jnp.float32), blank((padded, rows), jnp.bfloat16)),
        prepared,
        counts,
        acts,
        w_section,
    )
    even = lax.switch(
        jnp.where(section == 0, 0, 1 + section % 2),
        (
            lambda: (front[0], *updated(front[1], *parts, slots)),
            lambda: chain(near, slope, acts_t),
            nothing,
        ),
    )
    out = lax.switch(
        jnp.where(section == sections - 1, 2, section % 2),
        (lambda: even, lambda: chain(far, slope, acts_t), lambda: chain(around, slope, acts_t)),
    )
    return tuple(x[None] for x in out)


def solution(mesh):
    pipe = mesh.devices.shape[0]
    split = Mesh(mesh.devices.reshape(pipe, X_LO, COLUMNS), ("pipe", "x_lo", "y"))
    rows = ("x_lo", "y")
    in_specs = (
        P("pipe", rows, None),
        P("pipe", rows, None),
        P("pipe", None, None),
        P("pipe", rows, None),
        P("pipe", rows, None),
        P("pipe", rows, None),
        P(rows),
    )
    out_specs = (
        P("pipe", rows, None),
        P("pipe", rows, None),
        P("pipe", rows, None),
        P("pipe", rows, None),
    )
    return jax.shard_map(local, mesh=split, in_specs=in_specs, out_specs=out_specs, check_vma=False)
```

```python
import math

import jax
import jax.numpy as jnp
from jax import lax
from jax.experimental import pallas as pl
from jax.experimental.pallas import tpu as pltpu
from jax.sharding import Mesh
from jax.sharding import PartitionSpec as P


corr_first = 0.9999734386011124
corr_second = 0.09520785288696
X_LO = 2
COLUMNS = 8
SPACER = 8
HALVES = 2
VMEM = pl.BlockSpec(memory_space=pltpu.VMEM)


def prepare(counts_ref, acts_ref, w_ref, slope_ref, acts_t_ref):
    rows, width = acts_ref.shape
    batches = counts_ref.shape[0]
    block = rows // batches
    owned, stride = width // (X_LO * COLUMNS), width // COLUMNS + SPACER
    acts = acts_ref[...]
    acts_t = acts.T
    for y in range(COLUMNS):
        for x_lo in range(X_LO):
            to, at = y * stride + x_lo * owned, x_lo * (width // X_LO) + y * owned
            acts_t_ref[to : to + owned, :] = acts_t[at : at + owned, :]
        if y < COLUMNS - 1:
            acts_t_ref[y * stride + X_LO * owned : (y + 1) * stride, :] = jnp.zeros((SPACER, rows), acts.dtype)
    for b in range(batches):
        at = slice(b * block, (b + 1) * block)
        pre = jnp.dot(acts[at, :], w_ref[...], preferred_element_type=jnp.float32)
        _, back = jax.vjp(jax.nn.gelu, pre)
        live = lax.broadcasted_iota(jnp.int32, pre.shape, 0) < counts_ref[b]
        slope_ref[at, :] = jnp.where(live, back(jnp.ones_like(pre))[0], jnp.float32(0.0))


def local_terms(up_ref, slope_ref, acts_t_ref, w_ref, total_ref, in_grad_ref, held_w, held_out, sems):
    load = pltpu.make_async_copy(w_ref, held_w, sems.at[HALVES])
    load.start()
    lg = (up_ref[...].astype(jnp.float32) * slope_ref[...]).astype(jnp.bfloat16)
    total_ref[...] = jnp.dot(acts_t_ref[...], lg, preferred_element_type=jnp.float32).astype(jnp.bfloat16)
    load.wait()
    half = lg.shape[0] // HALVES
    stores = []
    for i in range(HALVES):
        at = slice(i * half, (i + 1) * half)
        held_out[at, :] = lax.dot_general(
            lg[at, :], held_w[...], (((1,), (1,)), ((), ())), preferred_element_type=jnp.float32
        ).astype(jnp.bfloat16)
        rows = pl.ds(i * half, half)
        stores.append(pltpu.make_async_copy(held_out.at[rows, :], in_grad_ref.at[rows, :], sems.at[i]))
        stores[-1].start()
    for store in stores:
        store.wait()


def unwritten(ref):
    del ref


def blank(shape, dtype):
    return pl.pallas_call(
        unwritten, out_shape=jax.ShapeDtypeStruct(shape, dtype), out_specs=pl.BlockSpec(memory_space=pl.ANY), name="blank"
    )()


def prepared(counts, acts, w_section):
    rows, width = acts.shape
    return pl.pallas_call(
        prepare,
        out_shape=(
            jax.ShapeDtypeStruct((rows, width), jnp.float32),
            jax.ShapeDtypeStruct((width + (COLUMNS - 1) * SPACER, rows), jnp.bfloat16),
        ),
        in_specs=[pl.BlockSpec(memory_space=pltpu.SMEM), VMEM, VMEM],
        out_specs=(VMEM, VMEM),
        compiler_params=pltpu.CompilerParams(vmem_limit_bytes=24 * 1024 * 1024),
        name="prepare",
    )(counts, acts, w_section)


def local_gradients(upstream, slope, acts_t, w_section):
    rows, width = upstream.shape
    anywhere = pl.BlockSpec(memory_space=pl.ANY)
    total, in_grad = pl.pallas_call(
        local_terms,
        out_shape=(
            jax.ShapeDtypeStruct((acts_t.shape[0], width), jnp.bfloat16),
            jax.ShapeDtypeStruct((rows, width), jnp.bfloat16),
        ),
        in_specs=[VMEM, VMEM, VMEM, anywhere],
        out_specs=(VMEM, anywhere),
        scratch_shapes=[
            pltpu.VMEM(w_section.shape, jnp.bfloat16),
            pltpu.VMEM((rows, width), jnp.bfloat16),
            pltpu.SemaphoreType.DMA((HALVES + 1,)),
        ],
        compiler_params=pltpu.CompilerParams(vmem_limit_bytes=24 * 1024 * 1024),
        name="local_terms",
    )(upstream, slope, acts_t, w_section)
    return in_grad, total


def updated(total, master_section, first, second, slots):
    owned = total.shape[1] // (X_LO * COLUMNS)
    along_y = lax.optimization_barrier(lax.psum_scatter(total, "y", scatter_dimension=0, tiled=True))
    x_lo, y = lax.axis_index("x_lo"), lax.axis_index("y")
    mine = lax.dynamic_slice_in_dim(along_y, y + x_lo * owned, owned, 0)
    other = lax.dynamic_slice_in_dim(along_y, y + (1 - x_lo) * owned, owned, 0)
    swapped = lax.dynamic_index_in_dim(lax.all_gather(other, "x_lo"), 1 - x_lo, 0, keepdims=False)
    summed = mine.astype(jnp.float32) + swapped.astype(jnp.float32)
    grad = summed * (1.0 / math.sqrt(slots))
    first_new = 0.9 * first + 0.1 * grad
    second_new = 0.999 * second + 0.001 * grad * grad
    direction = first_new / corr_first / (jnp.sqrt(second_new / corr_second) + 1e-08)
    master_out = master_section - 0.01 * (direction + 0.1 * master_section)
    return master_out, first_new, second_new


def local(saved, passed, weight, master, moment_one, moment_two, counts):
    acts, w_section, block = saved[0], weight[0], passed[0]
    rows, width = acts.shape
    sections = lax.axis_size("pipe")
    section = lax.axis_index("pipe")
    slots = X_LO * COLUMNS * rows
    parts = (master[0], moment_one[0], moment_two[0])
    padded = width + (COLUMNS - 1) * SPACER

    def chain(upstream, slope, acts_t):
        in_grad, total = local_gradients(upstream, slope, acts_t, w_section)
        return (in_grad, *updated(total, *parts, slots))

    def nothing():
        return (blank((rows, width), jnp.bfloat16), *(blank(p.shape, p.dtype) for p in parts))

    far = lax.ppermute(block, "pipe", [(s, s - 1) for s in range(2, sections, 2)])
    inputs = (counts, acts, w_section)
    ready = lax.cond(
        section == 1,
        prepared,
        lambda *_: (blank((rows, width), jnp.float32), blank((padded, rows), jnp.bfloat16)),
        *inputs,
    )
    own = lax.ppermute(block, "pipe", [(1, 0)])
    ready = lax.cond(section == 0, prepared, lambda *_: ready, *inputs)
    front = lax.cond(
        section == 0,
        lambda upstream: local_gradients(upstream, *ready, w_section),
        lambda _: (blank((rows, width), jnp.bfloat16), blank((padded, width), jnp.bfloat16)),
        own,
    )
    around = lax.ppermute(block, "pipe", [(0, sections - 1)])
    near = lax.ppermute(block, "pipe", [(s, s - 1) for s in range(3, sections, 2)])
    slope, acts_t = lax.cond(section <= 1, lambda *_: ready, prepared, *inputs)
    even = lax.switch(
        jnp.where(section == 0, 0, 1 + section % 2),
        (
            lambda: (front[0], *updated(front[1], *parts, slots)),
            lambda: chain(near, slope, acts_t),
            nothing,
        ),
    )
    out = lax.switch(
        jnp.where(section == sections - 1, 2, section % 2),
        (lambda: even, lambda: chain(far, slope, acts_t), lambda: chain(around, slope, acts_t)),
    )
    return tuple(x[None] for x in out)


def solution(mesh):
    pipe = mesh.devices.shape[0]
    split = Mesh(mesh.devices.reshape(pipe, X_LO, COLUMNS), ("pipe", "x_lo", "y"))
    rows = ("x_lo", "y")
    in_specs = (
        P("pipe", rows, None),
        P("pipe", rows, None),
        P("pipe", None, None),
        P("pipe", rows, None),
        P("pipe", rows, None),
        P("pipe", rows, None),
        P(rows),
    )
    out_specs = (
        P("pipe", rows, None),
        P("pipe", rows, None),
        P("pipe", rows, None),
        P("pipe", rows, None),
    )
    return jax.shard_map(local, mesh=split, in_specs=in_specs, out_specs=out_specs, check_vma=False)
```

```python
import math

import jax
import jax.numpy as jnp
from jax import lax
from jax.experimental import pallas as pl
from jax.experimental.pallas import tpu as pltpu
from jax.sharding import Mesh
from jax.sharding import PartitionSpec as P


corr_first = 0.9999734386011124
corr_second = 0.09520785288696
X_LO = 2
COLUMNS = 8
SPACER = 8
VMEM = pl.BlockSpec(memory_space=pltpu.VMEM)


def prepare(counts_ref, acts_ref, w_ref, slope_ref, acts_t_ref):
    rows, width = acts_ref.shape
    batches = counts_ref.shape[0]
    block = rows // batches
    owned, stride = width // (X_LO * COLUMNS), width // COLUMNS + SPACER
    acts = acts_ref[...]
    acts_t = acts.T
    for y in range(COLUMNS):
        for x_lo in range(X_LO):
            to, at = y * stride + x_lo * owned, x_lo * (width // X_LO) + y * owned
            acts_t_ref[to : to + owned, :] = acts_t[at : at + owned, :]
        if y < COLUMNS - 1:
            acts_t_ref[y * stride + X_LO * owned : (y + 1) * stride, :] = jnp.zeros((SPACER, rows), acts.dtype)
    for b in range(batches):
        at = slice(b * block, (b + 1) * block)
        pre = jnp.dot(acts[at, :], w_ref[...], preferred_element_type=jnp.float32)
        _, back = jax.vjp(jax.nn.gelu, pre)
        live = lax.broadcasted_iota(jnp.int32, pre.shape, 0) < counts_ref[b]
        slope_ref[at, :] = jnp.where(live, back(jnp.ones_like(pre))[0], jnp.float32(0.0))


def weight_term(up_ref, slope_ref, acts_t_ref, lg_ref, total_ref):
    lg = (up_ref[...].astype(jnp.float32) * slope_ref[...]).astype(jnp.bfloat16)
    lg_ref[...] = lg
    total_ref[...] = jnp.dot(acts_t_ref[...], lg, preferred_element_type=jnp.float32).astype(jnp.bfloat16)


def input_term(lg_ref, w_ref, in_grad_ref):
    in_grad_ref[...] = lax.dot_general(
        lg_ref[...], w_ref[...], (((1,), (1,)), ((), ())), preferred_element_type=jnp.float32
    ).astype(jnp.bfloat16)


def unwritten(ref):
    del ref


def blank(shape, dtype):
    return pl.pallas_call(
        unwritten, out_shape=jax.ShapeDtypeStruct(shape, dtype), out_specs=pl.BlockSpec(memory_space=pl.ANY), name="blank"
    )()


def prepared(counts, acts, w_section):
    rows, width = acts.shape
    return pl.pallas_call(
        prepare,
        out_shape=(
            jax.ShapeDtypeStruct((rows, width), jnp.float32),
            jax.ShapeDtypeStruct((width + (COLUMNS - 1) * SPACER, rows), jnp.bfloat16),
        ),
        in_specs=[pl.BlockSpec(memory_space=pltpu.SMEM), VMEM, VMEM],
        out_specs=(VMEM, VMEM),
        compiler_params=pltpu.CompilerParams(vmem_limit_bytes=24 * 1024 * 1024),
        name="prepare",
    )(counts, acts, w_section)


def weight_gradient(upstream, slope, acts_t):
    rows, width = upstream.shape
    return pl.pallas_call(
        weight_term,
        out_shape=(
            jax.ShapeDtypeStruct((rows, width), jnp.bfloat16),
            jax.ShapeDtypeStruct((acts_t.shape[0], width), jnp.bfloat16),
        ),
        in_specs=[VMEM] * 3,
        out_specs=(VMEM, VMEM),
        compiler_params=pltpu.CompilerParams(vmem_limit_bytes=24 * 1024 * 1024),
        name="weight_term",
    )(upstream, slope, acts_t)


def input_gradient(local_grad, w_section):
    rows, width = local_grad.shape
    return pl.pallas_call(
        input_term,
        out_shape=jax.ShapeDtypeStruct((rows, width), jnp.bfloat16),
        in_specs=[VMEM] * 2,
        out_specs=VMEM,
        cost_estimate=pl.CostEstimate(flops=2 * rows * width * width, bytes_accessed=3 << 20, transcendentals=0),
        compiler_params=pltpu.CompilerParams(vmem_limit_bytes=24 * 1024 * 1024),
        name="input_term",
    )(local_grad, w_section)


def updated(total, master_section, first, second, slots):
    owned = total.shape[1] // (X_LO * COLUMNS)
    along_y = lax.optimization_barrier(lax.psum_scatter(total, "y", scatter_dimension=0, tiled=True))
    x_lo, y = lax.axis_index("x_lo"), lax.axis_index("y")
    mine = lax.dynamic_slice_in_dim(along_y, y + x_lo * owned, owned, 0)
    other = lax.dynamic_slice_in_dim(along_y, y + (1 - x_lo) * owned, owned, 0)
    swapped = lax.dynamic_index_in_dim(lax.all_gather(other, "x_lo"), 1 - x_lo, 0, keepdims=False)
    summed = mine.astype(jnp.float32) + swapped.astype(jnp.float32)
    grad = summed * (1.0 / math.sqrt(slots))
    first_new = 0.9 * first + 0.1 * grad
    second_new = 0.999 * second + 0.001 * grad * grad
    direction = first_new / corr_first / (jnp.sqrt(second_new / corr_second) + 1e-08)
    master_out = master_section - 0.01 * (direction + 0.1 * master_section)
    return master_out, first_new, second_new


def local(saved, passed, weight, master, moment_one, moment_two, counts):
    acts, w_section, block = saved[0], weight[0], passed[0]
    rows, width = acts.shape
    sections = lax.axis_size("pipe")
    section = lax.axis_index("pipe")
    slots = X_LO * COLUMNS * rows
    parts = (master[0], moment_one[0], moment_two[0])
    padded = width + (COLUMNS - 1) * SPACER

    def chain(upstream, slope, acts_t):
        local_grad, total = weight_gradient(upstream, slope, acts_t)
        new = updated(total, *parts, slots)
        return (input_gradient(local_grad, w_section), *new)

    def front_of_first(upstream, slope, acts_t):
        local_grad, total = weight_gradient(upstream, slope, acts_t)
        return input_gradient(local_grad, w_section), total

    def nothing():
        return (blank((rows, width), jnp.bfloat16), *(blank(p.shape, p.dtype) for p in parts))

    far = lax.ppermute(block, "pipe", [(s, s - 1) for s in range(2, sections, 2)])
    inputs = (counts, acts, w_section)
    ready = lax.cond(
        section == 1,
        prepared,
        lambda *_: (blank((rows, width), jnp.float32), blank((padded, rows), jnp.bfloat16)),
        *inputs,
    )
    own = lax.ppermute(block, "pipe", [(1, 0)])
    ready = lax.cond(section == 0, prepared, lambda *_: ready, *inputs)
    front = lax.cond(
        section == 0,
        lambda upstream: front_of_first(upstream, *ready),
        lambda _: (blank((rows, width), jnp.bfloat16), blank((padded, width), jnp.bfloat16)),
        own,
    )
    around = lax.ppermute(block, "pipe", [(0, sections - 1)])
    near = lax.ppermute(block, "pipe", [(s, s - 1) for s in range(3, sections, 2)])
    slope, acts_t = lax.cond(section <= 1, lambda *_: ready, prepared, *inputs)
    even = lax.switch(
        jnp.where(section == 0, 0, 1 + section % 2),
        (
            lambda: (front[0], *updated(front[1], *parts, slots)),
            lambda: chain(near, slope, acts_t),
            nothing,
        ),
    )
    out = lax.switch(
        jnp.where(section == sections - 1, 2, section % 2),
        (lambda: even, lambda: chain(far, slope, acts_t), lambda: chain(around, slope, acts_t)),
    )
    return tuple(x[None] for x in out)


def solution(mesh):
    pipe = mesh.devices.shape[0]
    split = Mesh(mesh.devices.reshape(pipe, X_LO, COLUMNS), ("pipe", "x_lo", "y"))
    rows = ("x_lo", "y")
    in_specs = (
        P("pipe", rows, None),
        P("pipe", rows, None),
        P("pipe", None, None),
        P("pipe", rows, None),
        P("pipe", rows, None),
        P("pipe", rows, None),
        P(rows),
    )
    out_specs = (
        P("pipe", rows, None),
        P("pipe", rows, None),
        P("pipe", rows, None),
        P("pipe", rows, None),
    )
    return jax.shard_map(local, mesh=split, in_specs=in_specs, out_specs=out_specs, check_vma=False)
```
